32 devices in a mesh: dp: 32 (over z, y, x, core), mp: 1.
Axes of the slice: x: 2, y: 2, z: 4, core: 2. Of those that a mesh axis runs over, the one named last changes fastest.
Arguments:
- candidates: bfloat16 [32768, 256], P('dp', 'mp'), may hold values from 0 to 1, as said below
- first_weight: bfloat16 [256, 4096], P(None, 'mp'), may hold values from -48 to 48
- first_bias: bfloat16 [1, 4096], P(None, 'mp'), may hold values from -3 to 3
- second_weight: bfloat16 [4096, 4096], P(None, 'mp'), may hold values from -0.09375 to 0.09375
- second_bias: float32 [4096], P('mp'), may hold values from -3 to 3
- head_weight: float32 [4096], P('mp'), may hold values from -0.09375 to 0.09375
- owners: int32 [1024, 1], P('dp'), may hold values from 0 to 31; in each aligned block of 32 rows (0 to 31, 32 to 63, ...) at most 2 rows name the same one
Outputs:
- collected: bfloat16 [2048, 32, 256], P('dp', None, 'mp')
- collected_scores: bfloat16 [2048, 32], P('dp')
The draws below stay inside these ranges and needn't reach their ends.
Inputs may be any that keep to these rules, and one draw needn't show every extreme that they name: `candidates`: each row is nonnegative and sums to one. `owners`: among the 32 blocks of one index of dp no collector is named more than 2 times, a bound that some block reaches.
All inputs are finite; a program needn't handle non-finite values.
Results may differ from the reference program's by a relative error of at most 0.0033.
Values may be sent and summed in bfloat16 or wider, within the bound.
No kernel may reach another device: no remote copies, remote signals or barrier semaphores. Data moves between devices by JAX's collectives and lax.ppermute only.
A program may use at most 128 MiB of HBM per device.

```python
import math
import jax
import jax.numpy as jnp
import numpy as np
from jax import lax

DOM = 256
HID = 4096
BROWS = 32
PAIR = 2
NB = 32
ROWS_DEV = 1024
TOKENS = 32768
BLOCKS = 1024
SLOTS = 64
N_DP = 32


def draw_candidates(key, part):
    first_key, second_key = jax.random.split(jax.random.fold_in(key, 11))
    concentration = jax.random.uniform(first_key, (TOKENS, 1), minval=0.2, maxval=2.0)
    gammas = jax.random.gamma(second_key, concentration * jnp.ones((TOKENS, DOM), jnp.float32), (TOKENS, DOM))
    gammas = gammas.astype(jnp.float32)
    totals = jnp.sum(gammas, axis=1, keepdims=True)
    return (gammas / totals).astype(jnp.bfloat16)


def shared_out(stream_key, own, number, rows, count, top, bound, lean):
    ranking = jax.random.permutation(stream_key, count)
    heavy_load, ordinary = load_shares(count, rows * top, bound, lean, True), load_shares(count, rows * top, bound, lean, False)
    places = jnp.arange(count)

    def named(tallies, turn):
        used = int((tallies > 0).sum())
        fixed = max(1, used // 4)
        passed = fixed + (places - fixed + turn * (used - fixed)) % max(1, count - fixed)
        return jnp.zeros((count,), jnp.int32).at[ranking[jnp.where(places < fixed, places, passed)]].set(jnp.asarray(tallies, jnp.int32))

    tallies = jnp.where(number % 4 == 0, named(heavy_load, number // 4), named(ordinary, number - number // 4 - 1))
    mixed = jax.random.permutation(jax.random.fold_in(own, 3), count)
    giver, taker = mixed[0:count // 2 * 2:2], mixed[1:count // 2 * 2:2]
    room = jnp.minimum(tallies[giver] - 1, bound - tallies[taker]) // 2
    room = jnp.where((giver == ranking[0]) | (taker == ranking[0]) | (tallies[taker] == 0), 0, jnp.maximum(room, 0))
    passed = jax.random.randint(jax.random.fold_in(own, 4), (count // 2,), 0, 1 << 20) % (room + 1)
    tallies = tallies.at[giver].add(-passed).at[taker].add(passed)
    members = jnp.searchsorted(jnp.cumsum(tallies), jnp.arange(rows * top), side="right").astype(jnp.int32)
    table = members.reshape(top, rows).T
    table = table[jax.random.permutation(jax.random.fold_in(own, 1), rows)]
    turn = jax.random.randint(jax.random.fold_in(own, 2), (rows, 1), 0, top)
    return jnp.take_along_axis(table, (jnp.arange(top)[None, :] + turn) % top, axis=1)


def load_shares(amount, total, bound, lean, full):
    loads = [(1 << 20) // math.isqrt(standing ** lean) + 1 for standing in range(1, amount + 1)]
    largest = bound if full else min(bound, max(-(-total // amount), total * loads[0] // sum(loads)))
    least = 1 if total - largest >= amount - 1 else 0
    counts, surplus = [largest] + [least] * (amount - 1), total - largest - least * (amount - 1)
    while surplus > 0:
        free = [i for i in range(1, amount) if counts[i] < largest] or [i for i in range(1, amount) if counts[i] < bound]
        whole, left = sum([loads[i] for i in free]), surplus
        for i in free:
            addition = min(bound - counts[i], max(1, left * loads[i] // whole), surplus)
            counts[i] = counts[i] + addition
            surplus = surplus - addition
    return np.array(counts)


def scatter_about(key, extent, scale, most, kind=jnp.bfloat16):
    array = scale * jax.random.normal(key, extent, jnp.float32)
    return jnp.clip(array, min=-most, max=most).astype(kind)


def setup_inputs(seed: int = 0) -> dict:
    splits = jax.random.split(jax.random.key(seed), 8)
    candidates = draw_candidates(jax.random.fold_in(splits[7], 71), 0)
    first_weight = scatter_about(splits[1], (DOM, HID), 8.0, 48.0)
    first_bias = scatter_about(splits[2], (1, HID), 0.5, 3.0)
    second_weight = scatter_about(splits[3], (HID, HID), HID ** -0.5, 0.09375)
    second_bias = scatter_about(splits[4], (HID,), 0.5, 3.0, jnp.float32)
    head_weight = scatter_about(splits[5], (HID,), HID ** -0.5, 0.09375, jnp.float32)
    owners_keys = jax.random.split(jax.random.fold_in(splits[6], 1), BLOCKS // NB)
    owners_turns = jax.random.permutation(jax.random.fold_in(splits[6], 3), BLOCKS // NB)
    owners = jax.vmap(lambda own, number: shared_out(jax.random.fold_in(splits[6], 2), own, number, NB, N_DP, 1, PAIR, 2))(owners_keys, owners_turns).reshape((BLOCKS, 1))
    return {"candidates": candidates, "first_weight": first_weight, "first_bias": first_bias, "second_weight": second_weight, "second_bias": second_bias, "head_weight": head_weight, "owners": owners}


def score_group(group, first_weight, first_bias, second_weight, second_bias, head_weight):
    first = jnp.dot(group, first_weight, preferred_element_type=jnp.float32) + first_bias.astype(jnp.float32)
    hidden = jnp.maximum(first, 0.0).astype(jnp.bfloat16)
    second = jnp.dot(hidden, second_weight, preferred_element_type=jnp.float32) + second_bias
    second = jnp.maximum(second, 0.0)
    return jnp.dot(second, head_weight, precision=lax.Precision.HIGHEST)


def reference(candidates, first_weight, first_bias, second_weight, second_bias, head_weight, owners):
    grouped = candidates.reshape(N_DP, ROWS_DEV, DOM)
    scores = lax.map(lambda group: score_group(group, first_weight, first_bias, second_weight, second_bias, head_weight), grouped)
    scores = scores.reshape(BLOCKS, BROWS).astype(jnp.bfloat16)
    owner_list = owners[:, 0].reshape(N_DP, NB).astype(jnp.int32)
    same_owner = owner_list[:, :, None] == owner_list[:, None, :]
    before = lax.broadcasted_iota(jnp.int32, (NB, NB), 0) < lax.broadcasted_iota(jnp.int32, (NB, NB), 1)
    earlier_count = jnp.sum(jnp.where(same_owner & before[None, :, :], 1, 0), axis=1).astype(jnp.int32)
    group_index = lax.broadcasted_iota(jnp.int32, (N_DP, NB), 0)
    target = (owner_list * SLOTS + group_index * PAIR + earlier_count).reshape(-1).astype(jnp.int32)
    block_rows = candidates.reshape(BLOCKS, BROWS, DOM)
    collected = jnp.zeros((N_DP * SLOTS, BROWS, DOM), jnp.bfloat16).at[target].set(block_rows)
    collected_scores = jnp.zeros((N_DP * SLOTS, BROWS), jnp.bfloat16).at[target].set(scores)
    return collected, collected_scores
```

```python
import functools

import jax
import jax.numpy as jnp
from jax import lax
from jax.experimental import pallas as pl
from jax.experimental.pallas import tpu as pltpu
from jax.sharding import PartitionSpec as P


BROWS = 32
PAIR = 2
LANES = 128


def route_kernel(owners_ref, blocks_ref, out_ref, source_ref):
    block_count = blocks_ref.shape[0]
    slot_count = out_ref.shape[0]
    for s in range(slot_count):
        source_ref[s] = -1
    for b in range(block_count):
        first = owners_ref[b] * PAIR
        slot = first + jnp.where(source_ref[first] >= 0, 1, 0)
        source_ref[slot] = b

    def place(s, carry):
        source = source_ref[s]
        rows = blocks_ref[jnp.maximum(source, 0)]
        out_ref[s] = jnp.where(source >= 0, rows, jnp.zeros_like(rows))
        return carry

    lax.fori_loop(0, slot_count, place, 0, unroll=8)


def route(owner_list, candidates, collectors):
    rows, width = candidates.shape
    blocks = candidates.reshape(rows // BROWS, BROWS, width)
    slots = collectors * PAIR
    return pl.pallas_call(
        route_kernel,
        out_shape=jax.ShapeDtypeStruct((slots, BROWS, width), candidates.dtype),
        in_specs=[
            pl.BlockSpec(memory_space=pltpu.SMEM),
            pl.BlockSpec(memory_space=pltpu.VMEM),
        ],
        out_specs=pl.BlockSpec(memory_space=pltpu.VMEM),
        scratch_shapes=[pltpu.SMEM((slots,), jnp.int32)],
        name="route",
    )(owner_list, blocks)


def score_kernel(
    x_ref, w1_ref, b1_ref, w2_ref, b2_ref, head_ref, column_ref, row_ref,
    out_ref, hidden_ref, sums_ref, *, tile_m, tile_h,
):
    rows = x_ref.shape[0]
    width = w1_ref.shape[1]
    tile_n = w2_ref.shape[1]
    step = pl.program_id(0)

    @pl.when(step == 0)
    def _():
        sums_ref[...] = jnp.zeros_like(sums_ref)

        def first_layer(i, carry):
            at = pl.ds(pl.multiple_of(i * tile_h, tile_h), tile_h)
            first = jnp.dot(x_ref[...], w1_ref[:, at], preferred_element_type=jnp.float32)
            first = first + b1_ref[:, at].astype(jnp.float32)
            hidden_ref[:, at] = jnp.maximum(first, 0.0).astype(jnp.bfloat16)
            return carry

        lax.fori_loop(0, width // tile_h, first_layer, 0)

    for m in range(rows // tile_m):
        at = pl.ds(m * tile_m, tile_m)
        second = jnp.dot(hidden_ref[at, :], w2_ref[...], preferred_element_type=jnp.float32)
        weighted = jnp.maximum(second + b2_ref[...], 0.0) * head_ref[...]
        total = weighted[:, :LANES]
        for q in range(1, tile_n // LANES):
            total = total + weighted[:, q * LANES:(q + 1) * LANES]
        sums_ref[at, :] += total

    @pl.when(step == pl.num_programs(0) - 1)
    def _():
        blocks = rows // BROWS
        scores = jnp.sum(sums_ref[...].reshape(blocks, BROWS, LANES), axis=2)
        rounded = scores.astype(jnp.bfloat16)
        owner_row = row_ref[...]
        same_owner = column_ref[...] == owner_row
        before = lax.broadcasted_iota(jnp.int32, (blocks, blocks), 0) < lax.broadcasted_iota(
            jnp.int32, (blocks, blocks), 1
        )
        rank = jnp.sum(jnp.where(same_owner & before, 1, 0), axis=0, keepdims=True)
        target = owner_row * PAIR + rank
        collectors = out_ref.shape[0]
        for k in range(PAIR):
            slot = lax.broadcasted_iota(jnp.int32, (collectors, blocks), 0) * PAIR + k
            chooser = jnp.where(slot == target, 1.0, 0.0).astype(jnp.bfloat16)
            placed = jnp.dot(chooser, rounded, preferred_element_type=jnp.float32)
            out_ref[:, k, :] = placed.astype(out_ref.dtype)


def score(candidates, first_weight, first_bias, second_weight, second_bias, head_weight, owners, collectors):
    rows, domains = candidates.shape
    width = first_weight.shape[1]
    outs = second_weight.shape[1]
    blocks = owners.shape[0]
    tile_n, tile_m, tile_h = 512, 512, 512

    def whole(*shape):
        return pl.BlockSpec(shape, lambda j: (0,) * len(shape), pipeline_mode=pl.Buffered(1))

    return pl.pallas_call(
        functools.partial(score_kernel, tile_m=tile_m, tile_h=tile_h),
        out_shape=jax.ShapeDtypeStruct((collectors, PAIR, BROWS), jnp.bfloat16),
        grid=(outs // tile_n,),
        in_specs=[
            whole(rows, domains),
            whole(domains, width),
            whole(1, width),
            pl.BlockSpec((width, tile_n), lambda j: (0, j)),
            pl.BlockSpec((1, tile_n), lambda j: (0, j)),
            pl.BlockSpec((1, tile_n), lambda j: (0, j)),
            whole(blocks, 1),
            whole(1, blocks),
        ],
        out_specs=pl.BlockSpec((collectors, PAIR, BROWS), lambda j: (0, 0, 0)),
        scratch_shapes=[
            pltpu.VMEM((rows, width), jnp.bfloat16),
            pltpu.VMEM((rows, LANES), jnp.float32),
        ],
        compiler_params=pltpu.CompilerParams(vmem_limit_bytes=40 << 20),
        cost_estimate=pl.CostEstimate(
            flops=2 * rows * width * (domains + outs),
            transcendentals=0,
            bytes_accessed=2 * (rows * domains + domains * width + width * outs),
        ),
        name="score",
    )(
        candidates, first_weight, first_bias, second_weight, second_bias.reshape(1, -1),
        head_weight.reshape(1, -1), owners, owners.reshape(1, -1),
    )


def local(candidates, first_weight, first_bias, second_weight, second_bias, head_weight, owners):
    if lax.axis_size("mp") > 1:
        return split_local(
            candidates, first_weight, first_bias, second_weight, second_bias, head_weight, owners
        )
    collectors = lax.axis_size("dp")
    width = candidates.shape[1]
    outgoing = route(owners[:, 0], candidates, collectors)
    outgoing = outgoing.reshape(collectors, PAIR, BROWS, width)
    arrived = lax.all_to_all(outgoing, "dp", split_axis=0, concat_axis=0, tiled=True)
    outgoing_scores = score(
        candidates, first_weight, first_bias, second_weight, second_bias, head_weight, owners,
        collectors,
    )
    arrived, outgoing_scores = lax.optimization_barrier((arrived, outgoing_scores))
    arrived_scores = lax.all_to_all(outgoing_scores, "dp", split_axis=0, concat_axis=0, tiled=True)
    return (
        arrived.reshape(collectors * PAIR, BROWS, width),
        arrived_scores.reshape(collectors * PAIR, BROWS),
    )


def split_local(candidates, first_weight, first_bias, second_weight, second_bias, head_weight, owners):
    slice_width = candidates.shape[1]
    full_rows = lax.all_gather(candidates, "mp", axis=1, tiled=True)
    first_local = jnp.dot(
        full_rows, first_weight, preferred_element_type=jnp.float32
    ) + first_bias.astype(jnp.float32)
    hidden = jnp.maximum(first_local, 0.0).astype(jnp.bfloat16)
    second = jnp.dot(
        lax.all_gather(hidden, "mp", axis=1, tiled=True),
        second_weight,
        preferred_element_type=jnp.float32,
    )
    hidden_two = jnp.maximum(second + second_bias, 0.0)
    partial_score = jnp.dot(hidden_two, head_weight, precision=lax.Precision.HIGHEST)
    scores = lax.psum(partial_score, "mp")
    block_count = owners.shape[0]
    collectors = lax.axis_size("dp")
    owner_list = owners[:, 0]
    same_owner = owner_list[:, None] == owner_list[None, :]
    before = lax.broadcasted_iota(jnp.int32, (block_count, block_count), 0) < lax.broadcasted_iota(
        jnp.int32, (block_count, block_count), 1
    )
    earlier_count = jnp.sum(jnp.where(same_owner & before, 1, 0), axis=0).astype(jnp.int32)
    target = owner_list * PAIR + earlier_count
    slot_index = jnp.arange(collectors * PAIR, dtype=jnp.int32)
    chooser = slot_index[:, None] == target[None, :]
    block_rows = candidates.reshape(block_count, BROWS * slice_width)
    outgoing = jnp.dot(chooser.astype(jnp.bfloat16), block_rows, preferred_element_type=jnp.float32)
    outgoing = outgoing.astype(jnp.bfloat16).reshape(collectors, PAIR, BROWS, slice_width)
    score_blocks = scores.reshape(block_count, BROWS)
    outgoing_scores = jnp.dot(
        chooser.astype(jnp.float32), score_blocks, precision=lax.Precision.HIGHEST
    )
    outgoing_scores = outgoing_scores.astype(jnp.bfloat16).reshape(collectors, PAIR, BROWS)
    arrived, arrived_scores = (
        lax.all_to_all(outgoing, "dp", split_axis=0, concat_axis=0, tiled=True),
        lax.all_to_all(outgoing_scores, "dp", split_axis=0, concat_axis=0, tiled=True),
    )
    collected = arrived.reshape(collectors * PAIR, BROWS, slice_width)
    collected_scores = arrived_scores.reshape(collectors * PAIR, BROWS)
    return (collected, collected_scores)


def solution(mesh):
    placed = (
        P("dp", "mp"),
        P(None, "mp"),
        P(None, "mp"),
        P(None, "mp"),
        P("mp"),
        P("mp"),
        P("dp", None),
    )
    return jax.shard_map(
        local,
        mesh=mesh,
        in_specs=placed,
        out_specs=(P("dp", None, "mp"), P("dp", None)),
        check_vma=False,
    )
```

```python
import functools

import jax
import jax.numpy as jnp
from jax import lax
from jax.experimental import pallas as pl
from jax.experimental.pallas import tpu as pltpu
from jax.sharding import PartitionSpec as P


BROWS = 32
PAIR = 2
LANES = 128
VMEM_GRANT = (64 << 20) - (512 << 10)


def route_kernel(owners_ref, blocks_ref, out_ref, source_ref):
    block_count = blocks_ref.shape[0]
    slot_count = out_ref.shape[0]
    for s in range(slot_count):
        source_ref[s] = -1
    for b in range(block_count):
        first = owners_ref[b] * PAIR
        slot = first + jnp.where(source_ref[first] >= 0, 1, 0)
        source_ref[slot] = b

    def place(s, carry):
        source = source_ref[s]
        rows = blocks_ref[jnp.maximum(source, 0)]
        out_ref[s] = jnp.where(source >= 0, rows, jnp.zeros_like(rows))
        return carry

    lax.fori_loop(0, slot_count, place, 0, unroll=8)


def route(owner_list, candidates, collectors):
    rows, width = candidates.shape
    blocks = candidates.reshape(rows // BROWS, BROWS, width)
    slots = collectors * PAIR
    return pl.pallas_call(
        route_kernel,
        out_shape=jax.ShapeDtypeStruct((slots, BROWS, width), candidates.dtype),
        in_specs=[
            pl.BlockSpec(memory_space=pltpu.SMEM),
            pl.BlockSpec(memory_space=pltpu.VMEM),
        ],
        out_specs=pl.BlockSpec(memory_space=pltpu.VMEM),
        scratch_shapes=[pltpu.SMEM((slots,), jnp.int32)],
        name="route",
    )(owner_list, blocks)


def score_kernel(
    x_hbm, w1_hbm, b1_hbm, w2_hbm, b2_hbm, head_hbm, owners_hbm, out_ref,
    x_ref, w1_ref, b1_ref, w2_ref, b2_ref, head_ref, owners_ref, hidden_ref, sums_ref, chooser_ref,
    small_sem, w1_sem, w2_sem, *, tile_m, tile_h,
):
    rows = x_ref.shape[0]
    width = w1_ref.shape[1]
    slots, _, tile_n = w2_ref.shape
    tiles = w2_hbm.shape[1] // tile_n
    first_tiles = w1_sem.shape[0]
    columns = width // first_tiles
    blocks = rows // BROWS
    collectors = out_ref.shape[0]

    pairs = (
        (owners_hbm, owners_ref), (x_hbm, x_ref), (b1_hbm, b1_ref), (b2_hbm, b2_ref), (head_hbm, head_ref)
    )
    small = [pltpu.make_async_copy(a, b, small_sem.at[i]) for i, (a, b) in enumerate(pairs)]
    firsts = [
        pltpu.make_async_copy(
            w1_hbm.at[:, pl.ds(i * columns, columns)], w1_ref.at[:, pl.ds(i * columns, columns)], w1_sem.at[i]
        )
        for i in range(first_tiles)
    ]

    def load(j):
        at = pl.ds(pl.multiple_of(j * tile_n, tile_n), tile_n)
        return pltpu.make_async_copy(w2_hbm.at[:, at], w2_ref.at[j % slots], w2_sem.at[j % slots])

    for copy in small[:3] + firsts + small[3:]:
        copy.start()

    sums_ref[...] = jnp.zeros_like(sums_ref)
    small[0].wait()
    owner_row = jnp.broadcast_to(owners_ref[...], (blocks, blocks)).astype(jnp.float32)
    same_owner = owner_row == jnp.transpose(owner_row)
    before = lax.broadcasted_iota(jnp.int32, (blocks, blocks), 0) < lax.broadcasted_iota(
        jnp.int32, (blocks, blocks), 1
    )
    rank = jnp.sum(jnp.where(same_owner & before, 1.0, 0.0), axis=0, keepdims=True)
    target = owner_row[:1] * PAIR + rank
    for k in range(PAIR):
        slot = lax.broadcasted_iota(jnp.int32, (collectors, blocks), 0) * PAIR + k
        chooser_ref[k] = jnp.where(slot.astype(jnp.float32) == target, 1.0, 0.0).astype(jnp.bfloat16)

    small[1].wait()
    small[2].wait()
    for i, copy in enumerate(firsts):
        copy.wait()
        if i == 0:
            load(0).start()
        for q in range(columns // tile_h):
            at = pl.ds(i * columns + q * tile_h, tile_h)
            first = jnp.dot(x_ref[...], w1_ref[:, at], preferred_element_type=jnp.float32)
            first = first + b1_ref[:, at].astype(jnp.float32)
            hidden_ref[:, at] = jnp.maximum(first, 0.0).astype(jnp.bfloat16)
    small[3].wait()
    small[4].wait()

    def second_layer(j, carry):
        load(j).wait()

        @pl.when(j + 1 < tiles)
        def _():
            load(j + 1).start()

        columns_at = pl.ds(pl.multiple_of(j * tile_n, tile_n), tile_n)
        for m in range(rows // tile_m):
            at = pl.ds(m * tile_m, tile_m)
            second = jnp.dot(hidden_ref[at, :], w2_ref[j % slots], preferred_element_type=jnp.float32)
            weighted = jnp.maximum(second + b2_ref[:, columns_at], 0.0) * head_ref[:, columns_at]
            total = weighted[:, :LANES]
            for q in range(1, tile_n // LANES):
                total = total + weighted[:, q * LANES:(q + 1) * LANES]
            sums_ref[at, :] += total
        return carry

    lax.fori_loop(0, tiles, second_layer, 0)

    scores = jnp.sum(sums_ref[...].reshape(blocks, BROWS, LANES), axis=2)
    rounded = scores.astype(jnp.bfloat16)
    for k in range(PAIR):
        placed = jnp.dot(chooser_ref[k], rounded, preferred_element_type=jnp.float32)
        out_ref[:, k, :] = placed.astype(out_ref.dtype)


def score(candidates, first_weight, first_bias, second_weight, second_bias, head_weight, owners, collectors):
    rows, domains = candidates.shape
    width = first_weight.shape[1]
    outs = second_weight.shape[1]
    blocks = owners.shape[0]
    tile_n, tile_m, tile_h, first_tiles, slots = 512, 512, 512, 4, 2
    return pl.pallas_call(
        functools.partial(score_kernel, tile_m=tile_m, tile_h=tile_h),
        out_shape=jax.ShapeDtypeStruct((collectors, PAIR, BROWS), jnp.bfloat16),
        in_specs=[pl.BlockSpec(memory_space=pltpu.HBM)] * 7,
        out_specs=pl.BlockSpec(memory_space=pltpu.VMEM),
        scratch_shapes=[
            pltpu.VMEM((rows, domains), candidates.dtype),
            pltpu.VMEM((domains, width), first_weight.dtype),
            pltpu.VMEM((1, width), first_bias.dtype),
            pltpu.VMEM((slots, width, tile_n), second_weight.dtype),
            pltpu.VMEM((1, outs), second_bias.dtype),
            pltpu.VMEM((1, outs), head_weight.dtype),
            pltpu.VMEM((1, blocks), owners.dtype),
            pltpu.VMEM((rows, width), jnp.bfloat16),
            pltpu.VMEM((rows, LANES), jnp.float32),
            pltpu.VMEM((PAIR, collectors, blocks), jnp.bfloat16),
            pltpu.SemaphoreType.DMA((5,)),
            pltpu.SemaphoreType.DMA((first_tiles,)),
            pltpu.SemaphoreType.DMA((slots,)),
        ],
        compiler_params=pltpu.CompilerParams(vmem_limit_bytes=VMEM_GRANT),
        cost_estimate=pl.CostEstimate(
            flops=2 * rows * width * (domains + outs),
            transcendentals=0,
            bytes_accessed=2 * (rows * domains + domains * width + width * outs),
        ),
        name="score",
    )(
        candidates, first_weight, first_bias, second_weight, second_bias.reshape(1, -1),
        head_weight.reshape(1, -1), owners.reshape(1, -1),
    )


def settle_kernel(arrived_hbm, out_hbm, sems):
    parts = sems.shape[0]
    size = arrived_hbm.shape[0] // parts
    copies = [
        pltpu.make_async_copy(arrived_hbm.at[pl.ds(i * size, size)], out_hbm.at[pl.ds(i * size, size)], sems.at[i])
        for i in range(parts)
    ]
    for copy in copies:
        copy.start()
    for copy in copies:
        copy.wait()


def settle(arrived):
    return pl.pallas_call(
        settle_kernel,
        out_shape=jax.ShapeDtypeStruct(arrived.shape, arrived.dtype),
        in_specs=[pl.BlockSpec(memory_space=pltpu.HBM)],
        out_specs=pl.BlockSpec(memory_space=pltpu.HBM),
        scratch_shapes=[pltpu.SemaphoreType.DMA((8 if arrived.shape[0] % 8 == 0 else 1,))],
        name="settle",
    )(arrived)


def local(candidates, first_weight, first_bias, second_weight, second_bias, head_weight, owners):
    if lax.axis_size("mp") > 1:
        return split_local(
            candidates, first_weight, first_bias, second_weight, second_bias, head_weight, owners
        )
    collectors = lax.axis_size("dp")
    width = candidates.shape[1]
    outgoing = route(owners[:, 0], candidates, collectors)
    outgoing = outgoing.reshape(collectors, PAIR, BROWS, width)
    arrived = lax.all_to_all(outgoing, "dp", split_axis=0, concat_axis=0, tiled=True)
    outgoing_scores = score(
        candidates, first_weight, first_bias, second_weight, second_bias, head_weight, owners,
        collectors,
    )
    arrived, outgoing_scores = lax.optimization_barrier((arrived, outgoing_scores))
    arrived_scores = lax.all_to_all(outgoing_scores, "dp", split_axis=0, concat_axis=0, tiled=True)
    collected = settle(arrived.reshape(collectors * PAIR, BROWS, width))
    return (
        collected,
        arrived_scores.reshape(collectors * PAIR, BROWS),
    )


def split_local(candidates, first_weight, first_bias, second_weight, second_bias, head_weight, owners):
    slice_width = candidates.shape[1]
    full_rows = lax.all_gather(candidates, "mp", axis=1, tiled=True)
    first_local = jnp.dot(
        full_rows, first_weight, preferred_element_type=jnp.float32
    ) + first_bias.astype(jnp.float32)
    hidden = jnp.maximum(first_local, 0.0).astype(jnp.bfloat16)
    second = jnp.dot(
        lax.all_gather(hidden, "mp", axis=1, tiled=True),
        second_weight,
        preferred_element_type=jnp.float32,
    )
    hidden_two = jnp.maximum(second + second_bias, 0.0)
    partial_score = jnp.dot(hidden_two, head_weight, precision=lax.Precision.HIGHEST)
    scores = lax.psum(partial_score, "mp")
    block_count = owners.shape[0]
    collectors = lax.axis_size("dp")
    owner_list = owners[:, 0]
    same_owner = owner_list[:, None] == owner_list[None, :]
    before = lax.broadcasted_iota(jnp.int32, (block_count, block_count), 0) < lax.broadcasted_iota(
        jnp.int32, (block_count, block_count), 1
    )
    earlier_count = jnp.sum(jnp.where(same_owner & before, 1, 0), axis=0).astype(jnp.int32)
    target = owner_list * PAIR + earlier_count
    slot_index = jnp.arange(collectors * PAIR, dtype=jnp.int32)
    chooser = slot_index[:, None] == target[None, :]
    block_rows = candidates.reshape(block_count, BROWS * slice_width)
    outgoing = jnp.dot(chooser.astype(jnp.bfloat16), block_rows, preferred_element_type=jnp.float32)
    outgoing = outgoing.astype(jnp.bfloat16).reshape(collectors, PAIR, BROWS, slice_width)
    score_blocks = scores.reshape(block_count, BROWS)
    outgoing_scores = jnp.dot(
        chooser.astype(jnp.float32), score_blocks, precision=lax.Precision.HIGHEST
    )
    outgoing_scores = outgoing_scores.astype(jnp.bfloat16).reshape(collectors, PAIR, BROWS)
    arrived, arrived_scores = (
        lax.all_to_all(outgoing, "dp", split_axis=0, concat_axis=0, tiled=True),
        lax.all_to_all(outgoing_scores, "dp", split_axis=0, concat_axis=0, tiled=True),
    )
    collected = arrived.reshape(collectors * PAIR, BROWS, slice_width)
    collected_scores = arrived_scores.reshape(collectors * PAIR, BROWS)
    return (collected, collected_scores)


def solution(mesh):
    placed = (
        P("dp", "mp"),
        P(None, "mp"),
        P(None, "mp"),
        P(None, "mp"),
        P("mp"),
        P("mp"),
        P("dp", None),
    )
    return jax.shard_map(
        local,
        mesh=mesh,
        in_specs=placed,
        out_specs=(P("dp", None, "mp"), P("dp", None)),
        check_vma=False,
    )
```

```python
import functools

import jax
import jax.numpy as jnp
from jax import lax
from jax.experimental import pallas as pl
from jax.experimental.pallas import tpu as pltpu
from jax.sharding import PartitionSpec as P


BROWS = 32
PAIR = 2
LANES = 128
VMEM_GRANT = 36 << 20


def route_kernel(
    owners_ref, x_hbm, w1_hbm, b1_hbm, b2_hbm, head_hbm, row_hbm,
    out_hbm, x_ref, w1_ref, b1_ref, b2_ref, head_ref, row_ref,
    placed_ref, source_ref, in_sems, out_sems,
):
    parts = out_sems.shape[0]
    slot_count = placed_ref.shape[0]
    block_count = owners_ref.shape[0]
    copies = [
        pltpu.make_async_copy(a, b, in_sems.at[i])
        for i, (a, b) in enumerate(
            (
                (x_hbm, x_ref), (w1_hbm, w1_ref), (b1_hbm, b1_ref), (b2_hbm, b2_ref), (head_hbm, head_ref),
                (row_hbm, row_ref),
            )
        )
    ]
    for copy in copies:
        copy.start()
    for s in range(slot_count):
        source_ref[s] = -1
    for b in range(block_count):
        first = owners_ref[b] * PAIR
        slot = first + jnp.where(source_ref[first] >= 0, 1, 0)
        source_ref[slot] = b
    copies[0].wait()

    def place(s, carry):
        source = source_ref[s]
        rows = x_ref[pl.ds(pl.multiple_of(jnp.maximum(source, 0) * BROWS, BROWS), BROWS), :]
        placed_ref[s] = jnp.where(source >= 0, rows, jnp.zeros_like(rows))
        return carry

    size = slot_count // parts
    stores = []
    for i in range(parts):
        lax.fori_loop(i * size, (i + 1) * size, place, 0, unroll=8)
        at = pl.ds(i * size, size)
        store = pltpu.make_async_copy(placed_ref.at[at], out_hbm.at[at], out_sems.at[i])
        store.start()
        stores.append(store)
    for copy in stores + copies[1:]:
        copy.wait()


def route(owners, kept, collectors):
    candidates = kept[0]
    _, width = candidates.shape
    slots = collectors * PAIR
    parts = 4 if slots % 32 == 0 else 1
    hbm = pl.BlockSpec(memory_space=pltpu.HBM)
    vmem = pl.BlockSpec(memory_space=pltpu.VMEM)
    return pl.pallas_call(
        route_kernel,
        out_shape=[jax.ShapeDtypeStruct((slots, BROWS, width), candidates.dtype)]
        + [pltpu.VMEM(a.shape, a.dtype) for a in kept],
        in_specs=[pl.BlockSpec(memory_space=pltpu.SMEM)] + [hbm] * len(kept),
        out_specs=[hbm] + [vmem] * len(kept),
        scratch_shapes=[
            pltpu.VMEM((slots, BROWS, width), candidates.dtype),
            pltpu.SMEM((slots,), jnp.int32),
            pltpu.SemaphoreType.DMA((len(kept),)),
            pltpu.SemaphoreType.DMA((parts,)),
        ],
        name="route",
    )(owners[:, 0], *kept)


def score_kernel(
    x_ref, w1_ref, b1_ref, b2_ref, head_ref, owners_ref, w2_hbm, out_ref,
    w2_ref, hidden_ref, sums_ref, chooser_ref, w2_sem, *, tile_m, tile_h,
):
    rows = x_ref.shape[0]
    width = w1_ref.shape[1]
    slots, _, tile_n = w2_ref.shape
    tiles = w2_hbm.shape[1] // tile_n
    blocks = rows // BROWS
    collectors = out_ref.shape[0]

    def load(j):
        at = pl.ds(pl.multiple_of(j * tile_n, tile_n), tile_n)
        return pltpu.make_async_copy(w2_hbm.at[:, at], w2_ref.at[j % slots], w2_sem.at[j % slots])

    load(0).start()

    sums_ref[...] = jnp.zeros_like(sums_ref)
    for q in range(width // tile_h):
        at = pl.ds(q * tile_h, tile_h)
        first = jnp.dot(x_ref[...], w1_ref[:, at], preferred_element_type=jnp.float32)
        first = first + b1_ref[:, at].astype(jnp.float32)
        hidden_ref[:, at] = jnp.maximum(first, 0.0).astype(jnp.bfloat16)

    owner_row = jnp.broadcast_to(owners_ref[...], (blocks, blocks)).astype(jnp.float32)
    same_owner = owner_row == jnp.transpose(owner_row)
    before = lax.broadcasted_iota(jnp.int32, (blocks, blocks), 0) < lax.broadcasted_iota(
        jnp.int32, (blocks, blocks), 1
    )
    rank = jnp.sum(jnp.where(same_owner & before, 1.0, 0.0), axis=0, keepdims=True)
    target = owner_row[:1] * PAIR + rank
    for k in range(PAIR):
        slot = lax.broadcasted_iota(jnp.int32, (collectors, blocks), 0) * PAIR + k
        chooser_ref[k] = jnp.where(slot.astype(jnp.float32) == target, 1.0, 0.0).astype(jnp.bfloat16)

    def second_layer(j, carry):
        load(j).wait()

        @pl.when(j + 1 < tiles)
        def _():
            load(j + 1).start()

        columns_at = pl.ds(pl.multiple_of(j * tile_n, tile_n), tile_n)
        for m in range(rows // tile_m):
            at = pl.ds(m * tile_m, tile_m)
            second = jnp.dot(hidden_ref[at, :], w2_ref[j % slots], preferred_element_type=jnp.float32)
            weighted = jnp.maximum(second + b2_ref[:, columns_at], 0.0) * head_ref[:, columns_at]
            total = weighted[:, :LANES]
            for q in range(1, tile_n // LANES):
                total = total + weighted[:, q * LANES:(q + 1) * LANES]
            sums_ref[at, :] += total
        return carry

    lax.fori_loop(0, tiles, second_layer, 0)

    scores = jnp.sum(sums_ref[...].reshape(blocks, BROWS, LANES), axis=2)
    rounded = scores.astype(jnp.bfloat16)
    for k in range(PAIR):
        placed = jnp.dot(chooser_ref[k], rounded, preferred_element_type=jnp.float32)
        out_ref[:, k, :] = placed.astype(out_ref.dtype)


def score(kept, second_weight, collectors):
    candidates, first_weight = kept[:2]
    rows, domains = candidates.shape
    width = first_weight.shape[1]
    outs = second_weight.shape[1]
    blocks = rows // BROWS
    tile_n, tile_m, tile_h, slots = 512, 512, 512, 2
    return pl.pallas_call(
        functools.partial(score_kernel, tile_m=tile_m, tile_h=tile_h),
        out_shape=jax.ShapeDtypeStruct((collectors, PAIR, BROWS), jnp.bfloat16),
        in_specs=[pl.BlockSpec(memory_space=pltpu.VMEM)] * len(kept) + [pl.BlockSpec(memory_space=pltpu.HBM)],
        out_specs=pl.BlockSpec(memory_space=pltpu.VMEM),
        scratch_shapes=[
            pltpu.VMEM((slots, width, tile_n), second_weight.dtype),
            pltpu.VMEM((rows, width), jnp.bfloat16),
            pltpu.VMEM((rows, LANES), jnp.float32),
            pltpu.VMEM((PAIR, collectors, blocks), jnp.bfloat16),
            pltpu.SemaphoreType.DMA((slots,)),
        ],
        compiler_params=pltpu.CompilerParams(vmem_limit_bytes=VMEM_GRANT),
        cost_estimate=pl.CostEstimate(
            flops=2 * rows * width * (domains + outs),
            transcendentals=0,
            bytes_accessed=2 * (rows * domains + domains * width + width * outs),
        ),
        name="score",
    )(*kept, second_weight)


def settle_kernel(arrived_hbm, out_hbm, buffer_ref, in_sems, out_sems):
    parts = in_sems.shape[0]
    size = arrived_hbm.shape[0] // parts
    slices = [pl.ds(i * size, size) for i in range(parts)]
    fetches = [pltpu.make_async_copy(arrived_hbm.at[at], buffer_ref.at[at], in_sems.at[i]) for i, at in enumerate(slices)]
    stores = [pltpu.make_async_copy(buffer_ref.at[at], out_hbm.at[at], out_sems.at[i]) for i, at in enumerate(slices)]
    for fetch in fetches:
        fetch.start()
    for fetch, store in zip(fetches, stores):
        fetch.wait()
        store.start()
    for store in stores:
        store.wait()


def settle(arrived):
    parts = 4 if arrived.shape[0] % 4 == 0 else 1
    return pl.pallas_call(
        settle_kernel,
        out_shape=jax.ShapeDtypeStruct(arrived.shape, arrived.dtype),
        in_specs=[pl.BlockSpec(memory_space=pltpu.HBM)],
        out_specs=pl.BlockSpec(memory_space=pltpu.HBM),
        scratch_shapes=[
            pltpu.VMEM(arrived.shape, arrived.dtype),
            pltpu.SemaphoreType.DMA((parts,)),
            pltpu.SemaphoreType.DMA((parts,)),
        ],
        name="settle",
    )(arrived)


def local(candidates, first_weight, first_bias, second_weight, second_bias, head_weight, owners):
    if lax.axis_size("mp") > 1:
        return split_local(
            candidates, first_weight, first_bias, second_weight, second_bias, head_weight, owners
        )
    collectors = lax.axis_size("dp")
    width = candidates.shape[1]
    kept = (
        candidates, first_weight, first_bias, second_bias.reshape(1, -1), head_weight.reshape(1, -1),
        owners.reshape(1, -1),
    )
    outgoing, *kept = route(owners, kept, collectors)
    outgoing = outgoing.reshape(collectors, PAIR, BROWS, width)
    arrived = lax.all_to_all(outgoing, "dp", split_axis=0, concat_axis=0, tiled=True)
    outgoing_scores = score(kept, second_weight, collectors)
    arrived, outgoing_scores = lax.optimization_barrier((arrived, outgoing_scores))
    arrived_scores = lax.all_to_all(outgoing_scores, "dp", split_axis=0, concat_axis=0, tiled=True)
    collected = settle(arrived.reshape(collectors * PAIR, BROWS, width))
    return (
        collected,
        arrived_scores.reshape(collectors * PAIR, BROWS),
    )


def split_local(candidates, first_weight, first_bias, second_weight, second_bias, head_weight, owners):
    slice_width = candidates.shape[1]
    full_rows = lax.all_gather(candidates, "mp", axis=1, tiled=True)
    first_local = jnp.dot(
        full_rows, first_weight, preferred_element_type=jnp.float32
    ) + first_bias.astype(jnp.float32)
    hidden = jnp.maximum(first_local, 0.0).astype(jnp.bfloat16)
    second = jnp.dot(
        lax.all_gather(hidden, "mp", axis=1, tiled=True),
        second_weight,
        preferred_element_type=jnp.float32,
    )
    hidden_two = jnp.maximum(second + second_bias, 0.0)
    partial_score = jnp.dot(hidden_two, head_weight, precision=lax.Precision.HIGHEST)
    scores = lax.psum(partial_score, "mp")
    block_count = owners.shape[0]
    collectors = lax.axis_size("dp")
    owner_list = owners[:, 0]
    same_owner = owner_list[:, None] == owner_list[None, :]
    before = lax.broadcasted_iota(jnp.int32, (block_count, block_count), 0) < lax.broadcasted_iota(
        jnp.int32, (block_count, block_count), 1
    )
    earlier_count = jnp.sum(jnp.where(same_owner & before, 1, 0), axis=0).astype(jnp.int32)
    target = owner_list * PAIR + earlier_count
    slot_index = jnp.arange(collectors * PAIR, dtype=jnp.int32)
    chooser = slot_index[:, None] == target[None, :]
    block_rows = candidates.reshape(block_count, BROWS * slice_width)
    outgoing = jnp.dot(chooser.astype(jnp.bfloat16), block_rows, preferred_element_type=jnp.float32)
    outgoing = outgoing.astype(jnp.bfloat16).reshape(collectors, PAIR, BROWS, slice_width)
    score_blocks = scores.reshape(block_count, BROWS)
    outgoing_scores = jnp.dot(
        chooser.astype(jnp.float32), score_blocks, precision=lax.Precision.HIGHEST
    )
    outgoing_scores = outgoing_scores.astype(jnp.bfloat16).reshape(collectors, PAIR, BROWS)
    arrived, arrived_scores = (
        lax.all_to_all(outgoing, "dp", split_axis=0, concat_axis=0, tiled=True),
        lax.all_to_all(outgoing_scores, "dp", split_axis=0, concat_axis=0, tiled=True),
    )
    collected = arrived.reshape(collectors * PAIR, BROWS, slice_width)
    collected_scores = arrived_scores.reshape(collectors * PAIR, BROWS)
    return (collected, collected_scores)


def solution(mesh):
    placed = (
        P("dp", "mp"),
        P(None, "mp"),
        P(None, "mp"),
        P(None, "mp"),
        P("mp"),
        P("mp"),
        P("dp", None),
    )
    return jax.shard_map(
        local,
        mesh=mesh,
        in_specs=placed,
        out_specs=(P("dp", None, "mp"), P("dp", None)),
        check_vma=False,
    )
```

```python
import functools

import jax
import jax.numpy as jnp
from jax import lax
from jax.experimental import pallas as pl
from jax.experimental.pallas import tpu as pltpu
from jax.sharding import PartitionSpec as P


BROWS = 32
PAIR = 2
LANES = 128
VMEM_GRANT = 36 << 20
FIRST_STEPS = 2


def route_kernel(
    owners_ref, x_hbm, w1_hbm, b1_hbm, b2_hbm, head_hbm, row_hbm,
    out_hbm, x_ref, w1_ref, b1_ref, b2_ref, head_ref, row_ref,
    placed_ref, source_ref, in_sems, out_sems,
):
    parts = out_sems.shape[0]
    slot_count = placed_ref.shape[0]
    block_count = owners_ref.shape[0]
    copies = [
        pltpu.make_async_copy(a, b, in_sems.at[i])
        for i, (a, b) in enumerate(
            (
                (x_hbm, x_ref), (w1_hbm, w1_ref), (b1_hbm, b1_ref), (b2_hbm, b2_ref), (head_hbm, head_ref),
                (row_hbm, row_ref),
            )
        )
    ]
    for copy in copies:
        copy.start()
    for s in range(slot_count):
        source_ref[s] = -1
    for b in range(block_count):
        first = owners_ref[b] * PAIR
        slot = first + jnp.where(source_ref[first] >= 0, 1, 0)
        source_ref[slot] = b
    copies[0].wait()

    def place(s, carry):
        source = source_ref[s]
        rows = x_ref[pl.ds(pl.multiple_of(jnp.maximum(source, 0) * BROWS, BROWS), BROWS), :]
        placed_ref[s] = jnp.where(source >= 0, rows, jnp.zeros_like(rows))
        return carry

    size = slot_count // parts
    stores = []
    for i in range(parts):
        lax.fori_loop(i * size, (i + 1) * size, place, 0, unroll=8)
        at = pl.ds(i * size, size)
        store = pltpu.make_async_copy(placed_ref.at[at], out_hbm.at[at], out_sems.at[i])
        store.start()
        stores.append(store)
    for copy in stores + copies[1:]:
        copy.wait()


def route(owners, kept, collectors):
    candidates = kept[0]
    _, width = candidates.shape
    slots = collectors * PAIR
    parts = 4 if slots % 32 == 0 else 1
    hbm = pl.BlockSpec(memory_space=pltpu.HBM)
    vmem = pl.BlockSpec(memory_space=pltpu.VMEM)
    return pl.pallas_call(
        route_kernel,
        out_shape=[jax.ShapeDtypeStruct((slots, BROWS, width), candidates.dtype)]
        + [pltpu.VMEM(a.shape, a.dtype) for a in kept],
        in_specs=[pl.BlockSpec(memory_space=pltpu.SMEM)] + [hbm] * len(kept),
        out_specs=[hbm] + [vmem] * len(kept),
        scratch_shapes=[
            pltpu.VMEM((slots, BROWS, width), candidates.dtype),
            pltpu.SMEM((slots,), jnp.int32),
            pltpu.SemaphoreType.DMA((len(kept),)),
            pltpu.SemaphoreType.DMA((parts,)),
        ],
        name="route",
    )(owners[:, 0], *kept)


def score_kernel(
    x_ref, w1_ref, b1_ref, b2_ref, head_ref, owners_ref, w2_hbm, out_ref,
    w2_ref, hidden_ref, sums_ref, chooser_ref, w2_sem, *, tile_m, tile_h,
):
    rows = x_ref.shape[0]
    width = w1_ref.shape[1]
    slots, _, tile_n = w2_ref.shape
    tiles = w2_hbm.shape[1] // tile_n
    blocks = rows // BROWS
    collectors = out_ref.shape[0]

    def load(j):
        at = pl.ds(pl.multiple_of(j * tile_n, tile_n), tile_n)
        return pltpu.make_async_copy(w2_hbm.at[:, at], w2_ref.at[j % slots], w2_sem.at[j % slots])

    load(0).start()

    sums_ref[...] = jnp.zeros_like(sums_ref)

    def first_layer(i, carry):
        for q in range(width // tile_h // FIRST_STEPS):
            start = pl.multiple_of(i * (width // FIRST_STEPS) + q * tile_h, tile_h)
            at = pl.ds(start, tile_h)
            first = jnp.dot(x_ref[...], w1_ref[:, at], preferred_element_type=jnp.float32)
            first = first + b1_ref[:, at].astype(jnp.float32)
            hidden_ref[:, at] = jnp.maximum(first, 0.0).astype(jnp.bfloat16)
        return carry

    lax.fori_loop(0, FIRST_STEPS, first_layer, 0)

    owner_row = jnp.broadcast_to(owners_ref[...], (blocks, blocks)).astype(jnp.float32)
    same_owner = owner_row == jnp.transpose(owner_row)
    before = lax.broadcasted_iota(jnp.int32, (blocks, blocks), 0) < lax.broadcasted_iota(
        jnp.int32, (blocks, blocks), 1
    )
    rank = jnp.sum(jnp.where(same_owner & before, 1.0, 0.0), axis=0, keepdims=True)
    target = owner_row[:1] * PAIR + rank
    for k in range(PAIR):
        slot = lax.broadcasted_iota(jnp.int32, (collectors, blocks), 0) * PAIR + k
        chooser_ref[k] = jnp.where(slot.astype(jnp.float32) == target, 1.0, 0.0).astype(jnp.bfloat16)

    def second_layer(j, carry):
        load(j).wait()

        @pl.when(j + 1 < tiles)
        def _():
            load(j + 1).start()

        columns_at = pl.ds(pl.multiple_of(j * tile_n, tile_n), tile_n)
        for m in range(rows // tile_m):
            at = pl.ds(m * tile_m, tile_m)
            second = jnp.dot(hidden_ref[at, :], w2_ref[j % slots], preferred_element_type=jnp.float32)
            weighted = jnp.maximum(second + b2_ref[:, columns_at], 0.0) * head_ref[:, columns_at]
            total = weighted[:, :LANES]
            for q in range(1, tile_n // LANES):
                total = total + weighted[:, q * LANES:(q + 1) * LANES]
            sums_ref[at, :] += total
        return carry

    lax.fori_loop(0, tiles, second_layer, 0)

    scores = jnp.sum(sums_ref[...].reshape(blocks, BROWS, LANES), axis=2)
    rounded = scores.astype(jnp.bfloat16)
    for k in range(PAIR):
        placed = jnp.dot(chooser_ref[k], rounded, preferred_element_type=jnp.float32)
        out_ref[:, k, :] = placed.astype(out_ref.dtype)


def score(kept, second_weight, collectors):
    candidates, first_weight = kept[:2]
    rows, domains = candidates.shape
    width = first_weight.shape[1]
    outs = second_weight.shape[1]
    blocks = rows // BROWS
    tile_n, tile_m, tile_h, slots = 512, 512, 512, 2
    return pl.pallas_call(
        functools.partial(score_kernel, tile_m=tile_m, tile_h=tile_h),
        out_shape=jax.ShapeDtypeStruct((collectors, PAIR, BROWS), jnp.bfloat16),
        in_specs=[pl.BlockSpec(memory_space=pltpu.VMEM)] * len(kept) + [pl.BlockSpec(memory_space=pltpu.HBM)],
        out_specs=pl.BlockSpec(memory_space=pltpu.VMEM),
        scratch_shapes=[
            pltpu.VMEM((slots, width, tile_n), second_weight.dtype),
            pltpu.VMEM((rows, width), jnp.bfloat16),
            pltpu.VMEM((rows, LANES), jnp.float32),
            pltpu.VMEM((PAIR, collectors, blocks), jnp.bfloat16),
            pltpu.SemaphoreType.DMA((slots,)),
        ],
        compiler_params=pltpu.CompilerParams(vmem_limit_bytes=VMEM_GRANT),
        cost_estimate=pl.CostEstimate(
            flops=2 * rows * width * (domains + outs),
            transcendentals=0,
            bytes_accessed=2 * (rows * domains + domains * width + width * outs),
        ),
        name="score",
    )(*kept, second_weight)


def settle_kernel(arrived_hbm, out_hbm, buffer_ref, in_sems, out_sems):
    parts = in_sems.shape[0]
    size = arrived_hbm.shape[0] // parts
    slices = [pl.ds(i * size, size) for i in range(parts)]
    fetches = [pltpu.make_async_copy(arrived_hbm.at[at], buffer_ref.at[at], in_sems.at[i]) for i, at in enumerate(slices)]
    stores = [pltpu.make_async_copy(buffer_ref.at[at], out_hbm.at[at], out_sems.at[i]) for i, at in enumerate(slices)]
    for fetch in fetches:
        fetch.start()
    for fetch, store in zip(fetches, stores):
        fetch.wait()
        store.start()
    for store in stores:
        store.wait()


def settle(arrived):
    parts = 4 if arrived.shape[0] % 4 == 0 else 1
    return pl.pallas_call(
        settle_kernel,
        out_shape=jax.ShapeDtypeStruct(arrived.shape, arrived.dtype),
        in_specs=[pl.BlockSpec(memory_space=pltpu.HBM)],
        out_specs=pl.BlockSpec(memory_space=pltpu.HBM),
        scratch_shapes=[
            pltpu.VMEM(arrived.shape, arrived.dtype),
            pltpu.SemaphoreType.DMA((parts,)),
            pltpu.SemaphoreType.DMA((parts,)),
        ],
        name="settle",
    )(arrived)


def local(candidates, first_weight, first_bias, second_weight, second_bias, head_weight, owners):
    if lax.axis_size("mp") > 1:
        return split_local(
            candidates, first_weight, first_bias, second_weight, second_bias, head_weight, owners
        )
    collectors = lax.axis_size("dp")
    width = candidates.shape[1]
    kept = (
        candidates, first_weight, first_bias, second_bias.reshape(1, -1), head_weight.reshape(1, -1),
        owners.reshape(1, -1),
    )
    outgoing, *kept = route(owners, kept, collectors)
    outgoing = outgoing.reshape(collectors, PAIR, BROWS, width)
    arrived = lax.all_to_all(outgoing, "dp", split_axis=0, concat_axis=0, tiled=True)
    outgoing_scores = score(kept, second_weight, collectors)
    arrived, outgoing_scores = lax.optimization_barrier((arrived, outgoing_scores))
    arrived_scores = lax.all_to_all(outgoing_scores, "dp", split_axis=0, concat_axis=0, tiled=True)
    collected = settle(arrived.reshape(collectors * PAIR, BROWS, width))
    return (
        collected,
        arrived_scores.reshape(collectors * PAIR, BROWS),
    )


def split_local(candidates, first_weight, first_bias, second_weight, second_bias, head_weight, owners):
    slice_width = candidates.shape[1]
    full_rows = lax.all_gather(candidates, "mp", axis=1, tiled=True)
    first_local = jnp.dot(
        full_rows, first_weight, preferred_element_type=jnp.float32
    ) + first_bias.astype(jnp.float32)
    hidden = jnp.maximum(first_local, 0.0).astype(jnp.bfloat16)
    second = jnp.dot(
        lax.all_gather(hidden, "mp", axis=1, tiled=True),
        second_weight,
        preferred_element_type=jnp.float32,
    )
    hidden_two = jnp.maximum(second + second_bias, 0.0)
    partial_score = jnp.dot(hidden_two, head_weight, precision=lax.Precision.HIGHEST)
    scores = lax.psum(partial_score, "mp")
    block_count = owners.shape[0]
    collectors = lax.axis_size("dp")
    owner_list = owners[:, 0]
    same_owner = owner_list[:, None] == owner_list[None, :]
    before = lax.broadcasted_iota(jnp.int32, (block_count, block_count), 0) < lax.broadcasted_iota(
        jnp.int32, (block_count, block_count), 1
    )
    earlier_count = jnp.sum(jnp.where(same_owner & before, 1, 0), axis=0).astype(jnp.int32)
    target = owner_list * PAIR + earlier_count
    slot_index = jnp.arange(collectors * PAIR, dtype=jnp.int32)
    chooser = slot_index[:, None] == target[None, :]
    block_rows = candidates.reshape(block_count, BROWS * slice_width)
    outgoing = jnp.dot(chooser.astype(jnp.bfloat16), block_rows, preferred_element_type=jnp.float32)
    outgoing = outgoing.astype(jnp.bfloat16).reshape(collectors, PAIR, BROWS, slice_width)
    score_blocks = scores.reshape(block_count, BROWS)
    outgoing_scores = jnp.dot(
        chooser.astype(jnp.float32), score_blocks, precision=lax.Precision.HIGHEST
    )
    outgoing_scores = outgoing_scores.astype(jnp.bfloat16).reshape(collectors, PAIR, BROWS)
    arrived, arrived_scores = (
        lax.all_to_all(outgoing, "dp", split_axis=0, concat_axis=0, tiled=True),
        lax.all_to_all(outgoing_scores, "dp", split_axis=0, concat_axis=0, tiled=True),
    )
    collected = arrived.reshape(collectors * PAIR, BROWS, slice_width)
    collected_scores = arrived_scores.reshape(collectors * PAIR, BROWS)
    return (collected, collected_scores)


def solution(mesh):
    placed = (
        P("dp", "mp"),
        P(None, "mp"),
        P(None, "mp"),
        P(None, "mp"),
        P("mp"),
        P("mp"),
        P("dp", None),
    )
    return jax.shard_map(
        local,
        mesh=mesh,
        in_specs=placed,
        out_specs=(P("dp", None, "mp"), P("dp", None)),
        check_vma=False,
    )
```

```python
import functools

import jax
import jax.numpy as jnp
from jax import lax
from jax.experimental import pallas as pl
from jax.experimental.pallas import tpu as pltpu
from jax.sharding import PartitionSpec as P


BROWS = 32
PAIR = 2
LANES = 128
VMEM_GRANT = 44 << 20
FIRST_STEPS = 2
UNROLL = 3


def route_kernel(
    list_hbm, x_hbm, w1_hbm, b1_hbm, b2_hbm, head_hbm, row_hbm,
    out_hbm, x_ref, w1_ref, b1_ref, b2_ref, head_ref, row_ref,
    placed_ref, owners_ref, source_ref, list_sem, in_sems, out_sems,
):
    parts = out_sems.shape[0]
    slot_count = placed_ref.shape[0]
    block_count = owners_ref.shape[0]
    copies = [
        pltpu.make_async_copy(a, b, in_sems.at[i])
        for i, (a, b) in enumerate(
            (
                (x_hbm, x_ref), (w1_hbm, w1_ref), (b1_hbm, b1_ref), (b2_hbm, b2_ref), (head_hbm, head_ref),
                (row_hbm, row_ref),
            )
        )
    ]
    owner_copy = pltpu.make_async_copy(list_hbm, owners_ref, list_sem)
    owner_copy.start()
    for copy in copies:
        copy.start()
    for s in range(slot_count):
        source_ref[s] = -1
    owner_copy.wait()
    for b in range(block_count):
        first = owners_ref[b] * PAIR
        slot = first + jnp.where(source_ref[first] >= 0, 1, 0)
        source_ref[slot] = b
    copies[0].wait()

    def place(s, carry):
        source = source_ref[s]
        rows = x_ref[pl.ds(pl.multiple_of(jnp.maximum(source, 0) * BROWS, BROWS), BROWS), :]
        placed_ref[s] = jnp.where(source >= 0, rows, jnp.zeros_like(rows))
        return carry

    size = slot_count // parts
    stores = []
    for i in range(parts):
        lax.fori_loop(i * size, (i + 1) * size, place, 0, unroll=16)
        at = pl.ds(i * size, size)
        store = pltpu.make_async_copy(placed_ref.at[at], out_hbm.at[at], out_sems.at[i])
        store.start()
        stores.append(store)
    for copy in stores + copies[1:]:
        copy.wait()


def route(owners, kept, collectors):
    candidates = kept[0]
    rows, width = candidates.shape
    slots = collectors * PAIR
    parts = 2 if slots % 32 == 0 else 1
    hbm = pl.BlockSpec(memory_space=pltpu.HBM)
    vmem = pl.BlockSpec(memory_space=pltpu.VMEM)
    return pl.pallas_call(
        route_kernel,
        out_shape=[jax.ShapeDtypeStruct((slots, BROWS, width), candidates.dtype)]
        + [pltpu.VMEM(a.shape, a.dtype) for a in kept],
        in_specs=[hbm] * (1 + len(kept)),
        out_specs=[hbm] + [vmem] * len(kept),
        scratch_shapes=[
            pltpu.VMEM((slots, BROWS, width), candidates.dtype),
            pltpu.SMEM((rows // BROWS,), jnp.int32),
            pltpu.SMEM((slots,), jnp.int32),
            pltpu.SemaphoreType.DMA,
            pltpu.SemaphoreType.DMA((len(kept),)),
            pltpu.SemaphoreType.DMA((parts,)),
        ],
        name="route",
    )(owners[:, 0], *kept)


def score_kernel(
    x_ref, w1_ref, b1_ref, b2_ref, head_ref, owners_ref, w2_hbm, out_ref,
    w2_ref, hidden_ref, sums_ref, chooser_ref, w2_sem, *, tile_m, tile_h, singles, unroll,
):
    rows = x_ref.shape[0]
    width = w1_ref.shape[1]
    slots, _, tile_n = w2_ref.shape
    tiles = w2_hbm.shape[1] // tile_n
    blocks = rows // BROWS
    collectors = out_ref.shape[0]

    def load(j):
        at = pl.ds(pl.multiple_of(j * tile_n, tile_n), tile_n)
        return pltpu.make_async_copy(w2_hbm.at[:, at], w2_ref.at[j % slots], w2_sem.at[j % slots])

    load(0).start()

    sums_ref[...] = jnp.zeros_like(sums_ref)

    def first_layer(i, carry):
        for q in range(width // tile_h // FIRST_STEPS):
            start = pl.multiple_of(i * (width // FIRST_STEPS) + q * tile_h, tile_h)
            at = pl.ds(start, tile_h)
            first = jnp.dot(x_ref[...], w1_ref[:, at], preferred_element_type=jnp.float32)
            first = first + b1_ref[:, at].astype(jnp.float32)
            hidden_ref[:, at] = jnp.maximum(first, 0.0).astype(jnp.bfloat16)
        return carry

    lax.fori_loop(0, FIRST_STEPS, first_layer, 0)

    owner_row = jnp.broadcast_to(owners_ref[...], (blocks, blocks)).astype(jnp.float32)
    same_owner = owner_row == jnp.transpose(owner_row)
    before = lax.broadcasted_iota(jnp.int32, (blocks, blocks), 0) < lax.broadcasted_iota(
        jnp.int32, (blocks, blocks), 1
    )
    rank = jnp.sum(jnp.where(same_owner & before, 1.0, 0.0), axis=0, keepdims=True)
    target = owner_row[:1] * PAIR + rank
    for k in range(PAIR):
        slot = lax.broadcasted_iota(jnp.int32, (collectors, blocks), 0) * PAIR + k
        chooser_ref[k] = jnp.where(slot.astype(jnp.float32) == target, 1.0, 0.0).astype(jnp.bfloat16)

    def products(j):
        columns_at = pl.ds(pl.multiple_of(j * tile_n, tile_n), tile_n)
        for m in range(rows // tile_m):
            at = pl.ds(m * tile_m, tile_m)
            second = jnp.dot(hidden_ref[at, :], w2_ref[j % slots], preferred_element_type=jnp.float32)
            weighted = jnp.maximum(second + b2_ref[:, columns_at], 0.0) * head_ref[:, columns_at]
            total = weighted[:, :LANES]
            for q in range(1, tile_n // LANES):
                total = total + weighted[:, q * LANES:(q + 1) * LANES]
            sums_ref[at, :] += total

    def single(j, carry):
        load(j).wait()

        @pl.when(j + 1 < tiles)
        def _():
            load(j + 1).start()

        @pl.when(j == singles - 1)
        def _():
            for u in range(1, min(unroll, tiles - singles)):
                load(j + 1 + u).start()

        products(j)
        return carry

    def several(g, carry):
        base = singles + g * unroll
        for u in range(unroll):
            load(base + u).wait()

        @pl.when(base + unroll < tiles)
        def _():
            for u in range(unroll):
                load(base + unroll + u).start()

        for u in range(unroll):
            products(base + u)
        return carry

    lax.fori_loop(0, singles, single, 0)
    lax.fori_loop(0, (tiles - singles) // unroll, several, 0)

    scores = jnp.sum(sums_ref[...].reshape(blocks, BROWS, LANES), axis=2)
    rounded = scores.astype(jnp.bfloat16)
    for k in range(PAIR):
        placed = jnp.dot(chooser_ref[k], rounded, preferred_element_type=jnp.float32)
        out_ref[:, k, :] = placed.astype(out_ref.dtype)


def score(kept, second_weight, collectors):
    candidates, first_weight = kept[:2]
    rows, domains = candidates.shape
    width = first_weight.shape[1]
    outs = second_weight.shape[1]
    blocks = rows // BROWS
    tile_n, tile_m, tile_h, unroll = 512, 512, 512, UNROLL
    slots = 2 * unroll
    tiles = outs // tile_n
    singles = min(tiles, unroll - 1 + (tiles - unroll + 1) % unroll)
    return pl.pallas_call(
        functools.partial(score_kernel, tile_m=tile_m, tile_h=tile_h, singles=singles, unroll=unroll),
        out_shape=jax.ShapeDtypeStruct((collectors, PAIR, BROWS), jnp.bfloat16),
        in_specs=[pl.BlockSpec(memory_space=pltpu.VMEM)] * len(kept) + [pl.BlockSpec(memory_space=pltpu.HBM)],
        out_specs=pl.BlockSpec(memory_space=pltpu.VMEM),
        scratch_shapes=[
            pltpu.VMEM((slots, width, tile_n), second_weight.dtype),
            pltpu.VMEM((rows, width), jnp.bfloat16),
            pltpu.VMEM((rows, LANES), jnp.float32),
            pltpu.VMEM((PAIR, collectors, blocks), jnp.bfloat16),
            pltpu.SemaphoreType.DMA((slots,)),
        ],
        compiler_params=pltpu.CompilerParams(vmem_limit_bytes=VMEM_GRANT),
        cost_estimate=pl.CostEstimate(
            flops=2 * rows * width * (domains + outs),
            transcendentals=0,
            bytes_accessed=2 * (rows * domains + domains * width + width * outs),
        ),
        name="score",
    )(*kept, second_weight)


def settle_kernel(arrived_hbm, out_hbm, buffer_ref, in_sems, out_sems):
    parts = in_sems.shape[0]
    size = arrived_hbm.shape[0] // parts
    slices = [pl.ds(i * size, size) for i in range(parts)]
    fetches = [pltpu.make_async_copy(arrived_hbm.at[at], buffer_ref.at[at], in_sems.at[i]) for i, at in enumerate(slices)]
    stores = [pltpu.make_async_copy(buffer_ref.at[at], out_hbm.at[at], out_sems.at[i]) for i, at in enumerate(slices)]
    for fetch in fetches:
        fetch.start()
    for fetch, store in zip(fetches, stores):
        fetch.wait()
        store.start()
    for store in stores:
        store.wait()


def settle(arrived):
    parts = 4 if arrived.shape[0] % 4 == 0 else 1
    return pl.pallas_call(
        settle_kernel,
        out_shape=jax.ShapeDtypeStruct(arrived.shape, arrived.dtype),
        in_specs=[pl.BlockSpec(memory_space=pltpu.HBM)],
        out_specs=pl.BlockSpec(memory_space=pltpu.HBM),
        scratch_shapes=[
            pltpu.VMEM(arrived.shape, arrived.dtype),
            pltpu.SemaphoreType.DMA((parts,)),
            pltpu.SemaphoreType.DMA((parts,)),
        ],
        name="settle",
    )(arrived)


def local(candidates, first_weight, first_bias, second_weight, second_bias, head_weight, owners):
    if lax.axis_size("mp") > 1:
        return split_local(
            candidates, first_weight, first_bias, second_weight, second_bias, head_weight, owners
        )
    collectors = lax.axis_size("dp")
    width = candidates.shape[1]
    kept = (
        candidates, first_weight, first_bias, second_bias.reshape(1, -1), head_weight.reshape(1, -1),
        owners.reshape(1, -1),
    )
    outgoing, *kept = route(owners, kept, collectors)
    outgoing = outgoing.reshape(collectors, PAIR, BROWS, width)
    arrived = lax.all_to_all(outgoing, "dp", split_axis=0, concat_axis=0, tiled=True)
    outgoing_scores = score(kept, second_weight, collectors)
    arrived, outgoing_scores = lax.optimization_barrier((arrived, outgoing_scores))
    arrived_scores = lax.all_to_all(outgoing_scores, "dp", split_axis=0, concat_axis=0, tiled=True)
    collected = settle(arrived.reshape(collectors * PAIR, BROWS, width))
    return (
        collected,
        arrived_scores.reshape(collectors * PAIR, BROWS),
    )


def split_local(candidates, first_weight, first_bias, second_weight, second_bias, head_weight, owners):
    slice_width = candidates.shape[1]
    full_rows = lax.all_gather(candidates, "mp", axis=1, tiled=True)
    first_local = jnp.dot(
        full_rows, first_weight, preferred_element_type=jnp.float32
    ) + first_bias.astype(jnp.float32)
    hidden = jnp.maximum(first_local, 0.0).astype(jnp.bfloat16)
    second = jnp.dot(
        lax.all_gather(hidden, "mp", axis=1, tiled=True),
        second_weight,
        preferred_element_type=jnp.float32,
    )
    hidden_two = jnp.maximum(second + second_bias, 0.0)
    partial_score = jnp.dot(hidden_two, head_weight, precision=lax.Precision.HIGHEST)
    scores = lax.psum(partial_score, "mp")
    block_count = owners.shape[0]
    collectors = lax.axis_size("dp")
    owner_list = owners[:, 0]
    same_owner = owner_list[:, None] == owner_list[None, :]
    before = lax.broadcasted_iota(jnp.int32, (block_count, block_count), 0) < lax.broadcasted_iota(
        jnp.int32, (block_count, block_count), 1
    )
    earlier_count = jnp.sum(jnp.where(same_owner & before, 1, 0), axis=0).astype(jnp.int32)
    target = owner_list * PAIR + earlier_count
    slot_index = jnp.arange(collectors * PAIR, dtype=jnp.int32)
    chooser = slot_index[:, None] == target[None, :]
    block_rows = candidates.reshape(block_count, BROWS * slice_width)
    outgoing = jnp.dot(chooser.astype(jnp.bfloat16), block_rows, preferred_element_type=jnp.float32)
    outgoing = outgoing.astype(jnp.bfloat16).reshape(collectors, PAIR, BROWS, slice_width)
    score_blocks = scores.reshape(block_count, BROWS)
    outgoing_scores = jnp.dot(
        chooser.astype(jnp.float32), score_blocks, precision=lax.Precision.HIGHEST
    )
    outgoing_scores = outgoing_scores.astype(jnp.bfloat16).reshape(collectors, PAIR, BROWS)
    arrived, arrived_scores = (
        lax.all_to_all(outgoing, "dp", split_axis=0, concat_axis=0, tiled=True),
        lax.all_to_all(outgoing_scores, "dp", split_axis=0, concat_axis=0, tiled=True),
    )
    collected = arrived.reshape(collectors * PAIR, BROWS, slice_width)
    collected_scores = arrived_scores.reshape(collectors * PAIR, BROWS)
    return (collected, collected_scores)


def solution(mesh):
    placed = (
        P("dp", "mp"),
        P(None, "mp"),
        P(None, "mp"),
        P(None, "mp"),
        P("mp"),
        P("mp"),
        P("dp", None),
    )
    return jax.shard_map(
        local,
        mesh=mesh,
        in_specs=placed,
        out_specs=(P("dp", None, "mp"), P("dp", None)),
        check_vma=False,
    )
```

```python
import functools

import jax
import jax.numpy as jnp
from jax import lax
from jax.experimental import pallas as pl
from jax.experimental.pallas import tpu as pltpu
from jax.sharding import PartitionSpec as P


BROWS = 32
PAIR = 2
LANES = 128
VMEM_GRANT = 44 << 20
FIRST_STEPS = 2
UNROLL = 2


def route_kernel(
    list_hbm, x_hbm, w1_hbm, b1_hbm, b2_hbm, head_hbm, row_hbm,
    out_hbm, x_ref, w1_ref, b1_ref, b2_ref, head_ref, row_ref,
    placed_ref, owners_ref, source_ref, list_sem, in_sems, out_sems,
):
    parts = out_sems.shape[0]
    slot_count = placed_ref.shape[0]
    block_count = owners_ref.shape[0]
    copies = [
        pltpu.make_async_copy(a, b, in_sems.at[i])
        for i, (a, b) in enumerate(
            (
                (x_hbm, x_ref), (w1_hbm, w1_ref), (b1_hbm, b1_ref), (b2_hbm, b2_ref), (head_hbm, head_ref),
                (row_hbm, row_ref),
            )
        )
    ]
    owner_copy = pltpu.make_async_copy(list_hbm, owners_ref, list_sem)
    owner_copy.start()
    for copy in copies:
        copy.start()
    for s in range(slot_count):
        source_ref[s] = -1
    owner_copy.wait()
    for b in range(block_count):
        first = owners_ref[b] * PAIR
        slot = first + jnp.where(source_ref[first] >= 0, 1, 0)
        source_ref[slot] = b
    copies[0].wait()

    def place(s, carry):
        source = source_ref[s]
        rows = x_ref[pl.ds(pl.multiple_of(jnp.maximum(source, 0) * BROWS, BROWS), BROWS), :]
        placed_ref[s] = jnp.where(source >= 0, rows, jnp.zeros_like(rows))
        return carry

    size = slot_count // parts
    stores = []
    for i in range(parts):
        lax.fori_loop(i * size, (i + 1) * size, place, 0, unroll=8)
        at = pl.ds(i * size, size)
        store = pltpu.make_async_copy(placed_ref.at[at], out_hbm.at[at], out_sems.at[i])
        store.start()
        stores.append(store)
    for copy in stores + copies[1:]:
        copy.wait()


def route(owners, kept, collectors):
    candidates = kept[0]
    rows, width = candidates.shape
    slots = collectors * PAIR
    parts = 4 if slots % 32 == 0 else 1
    hbm = pl.BlockSpec(memory_space=pltpu.HBM)
    vmem = pl.BlockSpec(memory_space=pltpu.VMEM)
    return pl.pallas_call(
        route_kernel,
        out_shape=[jax.ShapeDtypeStruct((slots, BROWS, width), candidates.dtype)]
        + [pltpu.VMEM(a.shape, a.dtype) for a in kept],
        in_specs=[hbm] * (1 + len(kept)),
        out_specs=[hbm] + [vmem] * len(kept),
        scratch_shapes=[
            pltpu.VMEM((slots, BROWS, width), candidates.dtype),
            pltpu.SMEM((rows // BROWS,), jnp.int32),
            pltpu.SMEM((slots,), jnp.int32),
            pltpu.SemaphoreType.DMA,
            pltpu.SemaphoreType.DMA((len(kept),)),
            pltpu.SemaphoreType.DMA((parts,)),
        ],
        name="route",
    )(owners[:, 0], *kept)


def score_kernel(
    x_ref, w1_ref, b1_ref, b2_ref, head_ref, owners_ref, w2_hbm, out_ref,
    w2_ref, hidden_ref, sums_ref, chooser_ref, w2_sem, *, tile_m, tile_h, singles, unroll,
):
    rows = x_ref.shape[0]
    width = w1_ref.shape[1]
    slots, _, tile_n = w2_ref.shape
    tiles = w2_hbm.shape[1] // tile_n
    blocks = rows // BROWS
    collectors = out_ref.shape[0]

    def load(j):
        at = pl.ds(pl.multiple_of(j * tile_n, tile_n), tile_n)
        return pltpu.make_async_copy(w2_hbm.at[:, at], w2_ref.at[j % slots], w2_sem.at[j % slots])

    load(0).start()

    sums_ref[...] = jnp.zeros_like(sums_ref)

    owner_row = jnp.broadcast_to(owners_ref[...], (blocks, blocks)).astype(jnp.float32)
    same_owner = owner_row == jnp.transpose(owner_row)
    before = lax.broadcasted_iota(jnp.int32, (blocks, blocks), 0) < lax.broadcasted_iota(
        jnp.int32, (blocks, blocks), 1
    )
    rank = jnp.sum(jnp.where(same_owner & before, 1.0, 0.0), axis=0, keepdims=True)
    target = owner_row[:1] * PAIR + rank
    for k in range(PAIR):
        slot = lax.broadcasted_iota(jnp.int32, (collectors, blocks), 0) * PAIR + k
        chooser_ref[k] = jnp.where(slot.astype(jnp.float32) == target, 1.0, 0.0).astype(jnp.bfloat16)

    def first_layer(i, carry):
        for q in range(width // tile_h // FIRST_STEPS):
            start = pl.multiple_of(i * (width // FIRST_STEPS) + q * tile_h, tile_h)
            at = pl.ds(start, tile_h)
            first = jnp.dot(x_ref[...], w1_ref[:, at], preferred_element_type=jnp.float32)
            first = first + b1_ref[:, at].astype(jnp.float32)
            hidden_ref[:, at] = jnp.maximum(first, 0.0).astype(jnp.bfloat16)
        return carry

    lax.fori_loop(0, FIRST_STEPS, first_layer, 0)

    def products(j):
        columns_at = pl.ds(pl.multiple_of(j * tile_n, tile_n), tile_n)
        for m in range(rows // tile_m):
            at = pl.ds(m * tile_m, tile_m)
            second = jnp.dot(hidden_ref[at, :], w2_ref[j % slots], preferred_element_type=jnp.float32)
            weighted = jnp.maximum(second + b2_ref[:, columns_at], 0.0) * head_ref[:, columns_at]
            total = weighted[:, :LANES]
            for q in range(1, tile_n // LANES):
                total = total + weighted[:, q * LANES:(q + 1) * LANES]
            sums_ref[at, :] += total

    def single(j, carry):
        load(j).wait()

        @pl.when(j + 1 < tiles)
        def _():
            load(j + 1).start()

        @pl.when(j == singles - 1)
        def _():
            for u in range(1, min(unroll, tiles - singles)):
                load(j + 1 + u).start()

        products(j)
        return carry

    def several(g, carry):
        base = singles + g * unroll
        for u in range(unroll):
            load(base + u).wait()

        @pl.when(base + unroll < tiles)
        def _():
            for u in range(unroll):
                load(base + unroll + u).start()

        for u in range(unroll):
            products(base + u)
        return carry

    lax.fori_loop(0, singles, single, 0)
    lax.fori_loop(0, (tiles - singles) // unroll, several, 0)

    scores = jnp.sum(sums_ref[...].reshape(blocks, BROWS, LANES), axis=2)
    rounded = scores.astype(jnp.bfloat16)
    for k in range(PAIR):
        placed = jnp.dot(chooser_ref[k], rounded, preferred_element_type=jnp.float32)
        out_ref[:, k, :] = placed.astype(out_ref.dtype)


def score(kept, second_weight, collectors):
    candidates, first_weight = kept[:2]
    rows, domains = candidates.shape
    width = first_weight.shape[1]
    outs = second_weight.shape[1]
    blocks = rows // BROWS
    tile_n, tile_m, tile_h, unroll = 512, 512, 512, UNROLL
    slots = 2 * unroll
    tiles = outs // tile_n
    singles = min(tiles, unroll - 1 + (tiles - unroll + 1) % unroll)
    return pl.pallas_call(
        functools.partial(score_kernel, tile_m=tile_m, tile_h=tile_h, singles=singles, unroll=unroll),
        out_shape=jax.ShapeDtypeStruct((collectors, PAIR, BROWS), jnp.bfloat16),
        in_specs=[pl.BlockSpec(memory_space=pltpu.VMEM)] * len(kept) + [pl.BlockSpec(memory_space=pltpu.HBM)],
        out_specs=pl.BlockSpec(memory_space=pltpu.VMEM),
        scratch_shapes=[
            pltpu.VMEM((slots, width, tile_n), second_weight.dtype),
            pltpu.VMEM((rows, width), jnp.bfloat16),
            pltpu.VMEM((rows, LANES), jnp.float32),
            pltpu.VMEM((PAIR, collectors, blocks), jnp.bfloat16),
            pltpu.SemaphoreType.DMA((slots,)),
        ],
        compiler_params=pltpu.CompilerParams(vmem_limit_bytes=VMEM_GRANT),
        cost_estimate=pl.CostEstimate(
            flops=2 * rows * width * (domains + outs),
            transcendentals=0,
            bytes_accessed=2 * (rows * domains + domains * width + width * outs),
        ),
        name="score",
    )(*kept, second_weight)


def settle_kernel(arrived_hbm, out_hbm, buffer_ref, in_sems, out_sems):
    parts = in_sems.shape[0]
    size = arrived_hbm.shape[0] // parts
    slices = [pl.ds(i * size, size) for i in range(parts)]
    fetches = [pltpu.make_async_copy(arrived_hbm.at[at], buffer_ref.at[at], in_sems.at[i]) for i, at in enumerate(slices)]
    stores = [pltpu.make_async_copy(buffer_ref.at[at], out_hbm.at[at], out_sems.at[i]) for i, at in enumerate(slices)]
    for fetch in fetches:
        fetch.start()
    for fetch, store in zip(fetches, stores):
        fetch.wait()
        store.start()
    for store in stores:
        store.wait()


def settle(arrived):
    parts = 4 if arrived.shape[0] % 4 == 0 else 1
    return pl.pallas_call(
        settle_kernel,
        out_shape=jax.ShapeDtypeStruct(arrived.shape, arrived.dtype),
        in_specs=[pl.BlockSpec(memory_space=pltpu.HBM)],
        out_specs=pl.BlockSpec(memory_space=pltpu.HBM),
        scratch_shapes=[
            pltpu.VMEM(arrived.shape, arrived.dtype),
            pltpu.SemaphoreType.DMA((parts,)),
            pltpu.SemaphoreType.DMA((parts,)),
        ],
        name="settle",
    )(arrived)


def local(candidates, first_weight, first_bias, second_weight, second_bias, head_weight, owners):
    if lax.axis_size("mp") > 1:
        return split_local(
            candidates, first_weight, first_bias, second_weight, second_bias, head_weight, owners
        )
    collectors = lax.axis_size("dp")
    width = candidates.shape[1]
    kept = (
        candidates, first_weight, first_bias, second_bias.reshape(1, -1), head_weight.reshape(1, -1),
        owners.reshape(1, -1),
    )
    outgoing, *kept = route(owners, kept, collectors)
    outgoing = outgoing.reshape(collectors, PAIR, BROWS, width)
    arrived = lax.all_to_all(outgoing, "dp", split_axis=0, concat_axis=0, tiled=True)
    outgoing_scores = score(kept, second_weight, collectors)
    arrived, outgoing_scores = lax.optimization_barrier((arrived, outgoing_scores))
    arrived_scores = lax.all_to_all(outgoing_scores, "dp", split_axis=0, concat_axis=0, tiled=True)
    collected = settle(arrived.reshape(collectors * PAIR, BROWS, width))
    return (
        collected,
        arrived_scores.reshape(collectors * PAIR, BROWS),
    )


def split_local(candidates, first_weight, first_bias, second_weight, second_bias, head_weight, owners):
    slice_width = candidates.shape[1]
    full_rows = lax.all_gather(candidates, "mp", axis=1, tiled=True)
    first_local = jnp.dot(
        full_rows, first_weight, preferred_element_type=jnp.float32
    ) + first_bias.astype(jnp.float32)
    hidden = jnp.maximum(first_local, 0.0).astype(jnp.bfloat16)
    second = jnp.dot(
        lax.all_gather(hidden, "mp", axis=1, tiled=True),
        second_weight,
        preferred_element_type=jnp.float32,
    )
    hidden_two = jnp.maximum(second + second_bias, 0.0)
    partial_score = jnp.dot(hidden_two, head_weight, precision=lax.Precision.HIGHEST)
    scores = lax.psum(partial_score, "mp")
    block_count = owners.shape[0]
    collectors = lax.axis_size("dp")
    owner_list = owners[:, 0]
    same_owner = owner_list[:, None] == owner_list[None, :]
    before = lax.broadcasted_iota(jnp.int32, (block_count, block_count), 0) < lax.broadcasted_iota(
        jnp.int32, (block_count, block_count), 1
    )
    earlier_count = jnp.sum(jnp.where(same_owner & before, 1, 0), axis=0).astype(jnp.int32)
    target = owner_list * PAIR + earlier_count
    slot_index = jnp.arange(collectors * PAIR, dtype=jnp.int32)
    chooser = slot_index[:, None] == target[None, :]
    block_rows = candidates.reshape(block_count, BROWS * slice_width)
    outgoing = jnp.dot(chooser.astype(jnp.bfloat16), block_rows, preferred_element_type=jnp.float32)
    outgoing = outgoing.astype(jnp.bfloat16).reshape(collectors, PAIR, BROWS, slice_width)
    score_blocks = scores.reshape(block_count, BROWS)
    outgoing_scores = jnp.dot(
        chooser.astype(jnp.float32), score_blocks, precision=lax.Precision.HIGHEST
    )
    outgoing_scores = outgoing_scores.astype(jnp.bfloat16).reshape(collectors, PAIR, BROWS)
    arrived, arrived_scores = (
        lax.all_to_all(outgoing, "dp", split_axis=0, concat_axis=0, tiled=True),
        lax.all_to_all(outgoing_scores, "dp", split_axis=0, concat_axis=0, tiled=True),
    )
    collected = arrived.reshape(collectors * PAIR, BROWS, slice_width)
    collected_scores = arrived_scores.reshape(collectors * PAIR, BROWS)
    return (collected, collected_scores)


def solution(mesh):
    placed = (
        P("dp", "mp"),
        P(None, "mp"),
        P(None, "mp"),
        P(None, "mp"),
        P("mp"),
        P("mp"),
        P("dp", None),
    )
    return jax.shard_map(
        local,
        mesh=mesh,
        in_specs=placed,
        out_specs=(P("dp", None, "mp"), P("dp", None)),
        check_vma=False,
    )
```
